32 devices in a mesh: dp: 8 (over z, x), mp: 4 (over y, core).
Axes of the slice: x: 2, y: 2, z: 4, core: 2. Of those that a mesh axis runs over, the one named last changes fastest.
Arguments:
- tokens: bfloat16 [16384, 768], P(('dp', 'mp')), may hold values from -6 to 6
- cotangent: bfloat16 [16384, 768], P(('dp', 'mp')), may hold values from -6 to 6
- segment_ids: int32 [8, 2048], P('dp'), may hold values from 0 to 15, never falling along the last dimension, each value on 1 to 1024 neighbouring positions
- rand_blocks: int32 [8, 12, 30, 3], P('dp', 'mp'), may hold values from 1 to 30, as said below
- w_qkv: bfloat16 [3, 768, 768], P(None, 'dp', 'mp'), may hold values from -0.21875 to 0.21875
- qv_bias: bfloat16 [2, 768], P(None, 'mp'), may hold values from -1.1953125 to 1.1953125
- w_out: bfloat16 [768, 768], P('mp', 'dp'), may hold values from -1.75 to 1.75
- w_up: bfloat16 [768, 3072], P('dp', 'mp'), may hold values from -0.21875 to 0.21875
- up_bias: bfloat16 [3072], P('mp'), may hold values from -3 to 3
- w_down: bfloat16 [3072, 768], P('mp', 'dp'), may hold values from -0.109375 to 0.109375
- norm_gain: bfloat16 [2, 768], replicated, may hold values from 0.5 to 1.5
- norm_bias: bfloat16 [2, 768], replicated, may hold values from -1.796875 to 1.796875
- branch_bias: bfloat16 [2, 768], replicated, may hold values from -1.796875 to 1.796875
Outputs:
- layer_out: bfloat16 [16384, 768], P(('dp', 'mp'))
- input_grad: float32 [16384, 768], P(('dp', 'mp'))
- grad_qkv: float32 [3, 768, 768], P(None, 'dp', 'mp')
- grad_qv_bias: float32 [2, 768], P(None, 'mp')
- grad_out: float32 [768, 768], P('mp', 'dp')
- grad_up: float32 [768, 3072], P('dp', 'mp')
- grad_up_bias: float32 [3072], P('mp')
- grad_down: float32 [3072, 768], P('mp', 'dp')
- grad_norm_gain: float32 [2, 768], replicated
- grad_norm_bias: float32 [2, 768], replicated
- grad_branch_bias: float32 [2, 768], replicated
The draws below stay inside these ranges and needn't reach their ends.
Inputs may be any that keep to these rules, and one draw needn't show every extreme that they name: `rand_blocks`: entry [w, h, j - 1, :] serves query block j of window w and head h: its 3 blocks differ from one another and from 0, j - 1, j, j + 1 and 31.
All inputs are finite; a program needn't handle non-finite values.
Results may differ from the reference program's by a relative error of at most 0.017.
Values may be sent and summed in bfloat16 or wider, within the bound.
No kernel may reach another device: no remote copies, remote signals or barrier semaphores. Data moves between devices by JAX's collectives and lax.ppermute only.
A program may use at most 192 MiB of HBM per device.

```python
import math
from functools import partial
import jax
import jax.numpy as jnp
import numpy as np
from jax import lax

D = 768
HEADS = 12
HEAD_DIM = 64
FF = 3072
BLOCK = 64
RAND = 3
SEQ = 2048
NBLK = 32
WINDOWS = 8
TOKENS = 16384


def draw_rand_blocks(key, part):
    row_total = WINDOWS * HEADS * (NBLK - 2)
    row_keys = jax.random.split(key, row_total)

    def first_picks(row_key):
        return jax.random.permutation(row_key, NBLK - 5)[:RAND]
    picks = jax.vmap(first_picks)(row_keys).reshape(WINDOWS, HEADS, NBLK - 2, RAND).astype(jnp.int32)
    query_block = jnp.arange(1, NBLK - 1, dtype=jnp.int32)[None, None, :, None]
    return jnp.where(picks < query_block - 2, picks + 1, picks + 4).astype(jnp.int32)


def steps_of(own_key, shape, pieces, smallest, largest):
    def one(axis_at, shards_of):
        heights = jax.random.uniform(jax.random.fold_in(jax.random.fold_in(own_key, 6), axis_at), (shards_of,), jnp.float32, smallest / len(pieces), largest / len(pieces))
        return jnp.repeat(jnp.exp(heights), shape[axis_at] // shards_of).reshape((-1,) + (1,) * (len(shape) - axis_at - 1))

    gain = one(*pieces[0])
    for cut in pieces[1:]:
        gain = gain * one(*cut)
    return gain


def length_profile(number_of, total, reach, lean):
    loads = [(1 << 20) // math.isqrt(grade ** lean) + 1 for grade in range(2, number_of + 1)]
    surplus, counts = total - reach - (number_of - 1), [1] * (number_of - 1)
    while surplus > 0:
        free = [i for i in range(number_of - 1) if counts[i] < reach]
        mass, left = sum([loads[i] for i in free]), surplus
        for i in free:
            addition = min(reach - counts[i], max(1, left * loads[i] // mass), surplus)
            counts[i] = counts[i] + addition
            surplus = surplus - addition
    return np.array([reach] + counts)


def uneven_parts(stream_key, count, total, most, skew):
    if count == 2:
        one = jax.random.randint(stream_key, (), max(1, total - most), min(most, total - 1) + 1)
        return jnp.stack([one, total - one])
    tallies = jnp.asarray(length_profile(count, total, most, skew), jnp.int32)
    couples = (count - 1) // 2
    source_of, sink = tallies[1:1 + 2 * couples:2], tallies[2:2 + 2 * couples:2]
    room = jnp.minimum(source_of - 1, most - sink)
    passed = jax.random.randint(jax.random.fold_in(stream_key, 1), (couples,), 0, 1 << 20) % (room + 1)
    tallies = tallies.at[1:1 + 2 * couples:2].set(source_of - passed).at[2:2 + 2 * couples:2].set(sink + passed)
    return tallies[jax.random.permutation(jax.random.fold_in(stream_key, 2), count)]


def noise(own_key, extent, scale, most, shards=(), kind=jnp.bfloat16):
    values = scale * jax.random.normal(own_key, extent, jnp.float32)
    if shards:
        values = values * steps_of(own_key, extent, shards, -0.22, 0.18)
    return jnp.clip(values, -most, most).astype(kind)


def setup_inputs(seed: int = 0) -> dict:
    arg_keys = jax.random.split(jax.random.key(seed), 14)
    return {
        "tokens": noise(arg_keys[0], (TOKENS, D), 1.0, 6.0, ((0, 32),)),
        "cotangent": noise(arg_keys[1], (TOKENS, D), 1.0, 6.0, ((0, 32),)),
        "segment_ids": jax.vmap(lambda own: jnp.searchsorted(jnp.cumsum(uneven_parts(own, SEQ // (2 * BLOCK), SEQ, SEQ // 2, 2)), jnp.arange(SEQ), side="right"))(jax.random.split(arg_keys[2], WINDOWS)).reshape((WINDOWS, SEQ)).astype(jnp.int32),
        "rand_blocks": draw_rand_blocks(jax.random.fold_in(arg_keys[13], 71), 0),
        "w_qkv": noise(arg_keys[4], (3, D, D), D ** -0.5, 0.21875, ((1, 8), (2, 4))),
        "qv_bias": noise(arg_keys[5], (2, D), 0.2, 1.1953125, ((1, 4),)),
        "w_out": noise(arg_keys[6], (D, D), (D // 64) ** -0.5, 1.75, ((0, 4), (1, 8))),
        "w_up": noise(arg_keys[7], (D, FF), D ** -0.5, 0.21875, ((0, 8), (1, 4))),
        "up_bias": noise(arg_keys[8], (FF,), 0.5, 3.0, ((0, 4),)),
        "w_down": noise(arg_keys[9], (FF, D), FF ** -0.5, 0.109375, ((0, 4), (1, 8))),
        "norm_gain": jnp.clip(1.0 + 0.1 * jax.random.normal(arg_keys[10], (2, D), jnp.float32), 0.5, 1.5).astype(jnp.bfloat16),
        "norm_bias": noise(arg_keys[11], (2, D), 0.3, 1.796875),
        "branch_bias": noise(arg_keys[12], (2, D), 0.3, 1.796875),
    }


TOP_PRECISION = lax.Precision.HIGHEST
NEG_FILL = -1e+30
NORM_EPS = 1e-06

@jax.custom_vjp
def low(v):
    return lax.optimization_barrier(v.astype(jnp.bfloat16)).astype(jnp.float32)

@jax.custom_vjp
def low_back(v):
    return v

def low_keep(v):
    return (low(v), None)

def low_pass(kept, grad):
    return (grad,)

def back_keep(v):
    return (v, None)

def back_low(kept, grad):
    return (low(grad),)
low.defvjp(low_keep, low_pass)
low_back.defvjp(back_keep, back_low)

def matmul_high(left, right):
    return jnp.dot(left, right, precision=TOP_PRECISION, preferred_element_type=jnp.float32)

def layer_norm(values, gain_row, bias_row):
    average = lax.optimization_barrier(jnp.mean(values, axis=-1, keepdims=True))
    centered = values - average
    variance = lax.optimization_barrier(jnp.mean(centered * centered, axis=-1, keepdims=True))
    return centered * lax.rsqrt(variance + NORM_EPS) * gain_row + bias_row

def block_layout(rand_head):
    middle = jnp.arange(1, NBLK - 1, dtype=jnp.int32)
    fixed_index = jnp.stack([jnp.zeros_like(middle), jnp.full_like(middle, NBLK - 1), middle - 1, middle, middle + 1], axis=1)
    key_index = jnp.concatenate([fixed_index, rand_head.astype(jnp.int32)], axis=1)
    column = jnp.arange(5 + RAND, dtype=jnp.int32)[None, :]
    repeated = (column == 2) & (middle[:, None] == 1) | (column == 4) & (middle[:, None] == NBLK - 2)
    return (key_index, jnp.logical_not(repeated))

def softmax_under_mask(scores, permitted_mask):
    scores = low_back(jnp.where(permitted_mask, scores, NEG_FILL))
    return low(jax.nn.softmax(scores, axis=-1))

def head_attention(segment_row, inputs):
    query_head, key_head, value_head, rand_head = inputs
    score_scale = 1.0 / math.sqrt(HEAD_DIM)
    key_index, slot_ok = block_layout(rand_head)
    seg_blocks = segment_row.reshape(NBLK, BLOCK)
    seg_keys = seg_blocks[key_index].reshape(NBLK - 2, -1)
    slot_mask = jnp.repeat(slot_ok, BLOCK, axis=1)
    permitted_mask = (seg_blocks[1:-1][:, :, None] == seg_keys[:, None, :]) & slot_mask[:, None, :]
    blocked_queries = query_head.reshape(NBLK, BLOCK, HEAD_DIM)
    selected_keys = key_head.reshape(NBLK, BLOCK, HEAD_DIM)[key_index].reshape(NBLK - 2, -1, HEAD_DIM)
    selected_values = value_head.reshape(NBLK, BLOCK, HEAD_DIM)[key_index].reshape(NBLK - 2, -1, HEAD_DIM)
    central_scores = jnp.einsum('pwv,pxv->pwx', blocked_queries[1:-1], selected_keys, precision=TOP_PRECISION) * score_scale
    central_output = jnp.einsum('izl,ilg->izg', softmax_under_mask(central_scores, permitted_mask), selected_values, precision=TOP_PRECISION)
    edge_query = jnp.concatenate([blocked_queries[0], blocked_queries[-1]], axis=0)
    edge_seg = jnp.concatenate([seg_blocks[0], seg_blocks[-1]], axis=0)
    edge_scores = matmul_high(edge_query, key_head.T) * score_scale
    edge_out = matmul_high(softmax_under_mask(edge_scores, edge_seg[:, None] == segment_row[None, :]), value_head)
    return jnp.concatenate([edge_out[:BLOCK], central_output.reshape(-1, HEAD_DIM), edge_out[BLOCK:]], axis=0)

def window_forward(segment_row, rand_window, window_rows, w_qkv, qv_bias, w_out, w_up, up_bias, w_down, norm_gain, norm_bias, branch_bias):
    act_one = low(layer_norm(window_rows, norm_gain[0], norm_bias[0]))
    queries = low(low_back(matmul_high(act_one, w_qkv[0]) + qv_bias[0]))
    keys = low(low_back(matmul_high(act_one, w_qkv[1])))
    values = low(low_back(matmul_high(act_one, w_qkv[2]) + qv_bias[1]))

    def by_head(matrix):
        return matrix.reshape(SEQ, HEADS, HEAD_DIM).transpose(1, 0, 2)
    attention = jax.checkpoint(partial(head_attention, segment_row))
    attended = lax.map(attention, (by_head(queries), by_head(keys), by_head(values), rand_window))
    merged = low(low_back(attended.transpose(1, 0, 2).reshape(SEQ, D)))
    hidden = window_rows + low_back(matmul_high(merged, w_out)) + branch_bias[0]
    act_two = low(layer_norm(hidden, norm_gain[1], norm_bias[1]))
    pre_act = low_back(matmul_high(act_two, w_up) + up_bias)
    activ = low(jax.nn.gelu(pre_act, approximate=False))
    return hidden + low_back(matmul_high(activ, w_down)) + branch_bias[1]

def reference(tokens, cotangent, segment_ids, rand_blocks, w_qkv, qv_bias, w_out, w_up, up_bias, w_down, norm_gain, norm_bias, branch_bias):
    weights = (w_qkv.astype(jnp.float32), qv_bias.astype(jnp.float32), w_out.astype(jnp.float32), w_up.astype(jnp.float32), up_bias.astype(jnp.float32), w_down.astype(jnp.float32), norm_gain.astype(jnp.float32), norm_bias.astype(jnp.float32), branch_bias.astype(jnp.float32))

    def one_window(running, window):
        window_rows, window_grad, segment_row, rand_window = window
        forward = partial(window_forward, segment_row, rand_window)
        result, pullback = jax.vjp(forward, window_rows.astype(jnp.float32), *weights)
        gradients = pullback(window_grad.astype(jnp.float32))
        running = tuple((summed + grad_part for summed, grad_part in zip(running, gradients[1:])))
        return (running, (result.astype(jnp.bfloat16), gradients[0]))
    initial = tuple((jnp.zeros_like(weight) for weight in weights))
    running, (outputs, input_grad) = lax.scan(one_window, initial, (tokens.reshape(WINDOWS, SEQ, D), cotangent.reshape(WINDOWS, SEQ, D), segment_ids, rand_blocks))
    return (outputs.reshape(TOKENS, D), input_grad.reshape(TOKENS, D), running[0], running[1], running[2], running[3], running[4], running[5], running[6], running[7], running[8])
```

```python
import functools

import jax
import jax.numpy as jnp
from jax import lax
from jax.experimental import pallas as pl
from jax.experimental.pallas import tpu as pltpu
from jax.sharding import PartitionSpec as P

HEAD_DIM = 64
BLOCK = 64
CHUNK = 512
SLOTS = 8
NEG_FILL = -1e30
NORM_EPS = 1e-06
INV_ROOT_TWO = 0.7071067811865476
INV_ROOT_TWO_PI = 0.3989422804014327
SCALE = 0.125

NN = (((1,), (0,)), ((), ()))
NT = (((1,), (1,)), ((), ()))
TN = (((0,), (0,)), ((), ()))


def dot(left, right, dims=NN):
    return lax.dot_general(left, right, dims, preferred_element_type=jnp.float32)


def low(v):
    return v.astype(jnp.bfloat16)


def wide(v):
    return v.astype(jnp.float32)


def slot_blocks(rand_ref, head, j, nblk):
    base = (head * (nblk - 2) + (j - 1)) * 3
    return [0, nblk - 1, j - 1, j, j + 1] + [rand_ref[base + t] for t in range(3)]


def slot_segments(segtab_ref, blocks, j, nblk):
    left = lax.broadcasted_iota(jnp.int32, (1, 128), 1) < BLOCK
    rows = []
    for s, b in enumerate(blocks):
        row = segtab_ref[pl.ds(b, 1), :]
        if s == 2:
            row = jnp.where(j == 1, -1, row)
        if s == 4:
            row = jnp.where(j == nblk - 2, -1, row)
        rows.append(row)
    return jnp.concatenate(
        [jnp.where(left, rows[2 * i], rows[2 * i + 1]) for i in range(SLOTS // 2)], axis=1
    )


def tile4(v):
    return jnp.concatenate([v] * 4, axis=1)


class Half:
    def __init__(self, meta_ref, other, nblk):
        self.flip = meta_ref[0]
        self.chip = meta_ref[1] ^ other
        self.base = other * (nblk // 2)
        self.nblk = nblk

    def place(self, block):
        return pl.multiple_of((block ^ self.flip) * BLOCK, BLOCK)

    def middle(self, i):
        return self.chip * (self.nblk // 2 - 1) + 1 + i

    def edge(self):
        return self.chip * (self.nblk - 1)

    def local(self, block):
        return pl.multiple_of(((block ^ self.flip) - self.base) * BLOCK, BLOCK)


def fwd_kernel(
    meta_ref, rand_ref, q_ref, kv_ref, segq_ref, segtab_ref, segrow_ref,
    o_ref, lse_ref, s_ref, p_ref, l_ref, *, nblk, other,
):
    head = pl.program_id(0)
    half = Half(meta_ref, other, nblk)
    count = nblk // 2 - 1
    chunks = nblk * BLOCK // CHUNK
    top = count * BLOCK

    def gather(j):
        blocks = slot_blocks(rand_ref, head, j, nblk)
        keys = jnp.concatenate([kv_ref[pl.ds(half.place(b), BLOCK), :] for b in blocks], axis=0)
        return blocks, keys

    def segq_of(j):
        return tile4(segq_ref[pl.ds(pl.multiple_of(j * BLOCK, BLOCK), BLOCK), :])

    def score(i, c):
        j = half.middle(i)
        blocks, keys = gather(j)
        s = dot(q_ref[pl.ds(half.place(j), BLOCK), :], keys, NT)
        ok = segq_of(j) == slot_segments(segtab_ref, blocks, j, nblk)
        s_ref[pl.ds(pl.multiple_of(i * BLOCK, BLOCK), BLOCK), :] = jnp.where(ok, s, NEG_FILL)
        return c

    lax.fori_loop(0, count, score, 0, unroll=count)
    edge = half.edge()
    q_edge = q_ref[pl.ds(half.place(edge), BLOCK), :]
    seg_edge = segq_of(edge)
    for c in range(chunks):
        s = dot(q_edge, kv_ref[c * CHUNK : (c + 1) * CHUNK, :], NT)
        seg = segrow_ref[pl.ds(c ^ meta_ref[2], 1), :]
        s_ref[top + c * BLOCK : top + (c + 1) * BLOCK, :] = jnp.where(seg_edge == seg, s, NEG_FILL)

    def soften(i, c):
        rows = pl.ds(pl.multiple_of(i * BLOCK, BLOCK), BLOCK)
        s = s_ref[rows, :]
        peak = jnp.max(s, axis=1, keepdims=True)
        p = jnp.exp(s - peak)
        total = jnp.sum(p, axis=1, keepdims=True)
        p_ref[rows, :] = low(p)
        l_ref[rows, :] = jnp.broadcast_to(1.0 / total, (BLOCK, 128))
        lse_ref[pl.ds(half.local(half.middle(i)), BLOCK), :] = jnp.broadcast_to(
            peak + jnp.log(total), (BLOCK, 128)
        )
        return c

    lax.fori_loop(0, count, soften, 0, unroll=count)
    peak = s_ref[top : top + BLOCK, :]
    for c in range(1, chunks):
        peak = jnp.maximum(peak, s_ref[top + c * BLOCK : top + (c + 1) * BLOCK, :])
    peak = jnp.max(peak, axis=1, keepdims=True)
    total = jnp.zeros((BLOCK, CHUNK), jnp.float32)
    for c in range(chunks):
        p = jnp.exp(s_ref[top + c * BLOCK : top + (c + 1) * BLOCK, :] - peak)
        p_ref[top + c * BLOCK : top + (c + 1) * BLOCK, :] = low(p)
        total = total + p
    total = jnp.sum(total, axis=1, keepdims=True)
    out = jnp.zeros((BLOCK, 128), jnp.float32)
    for c in range(chunks):
        out = out + dot(
            p_ref[top + c * BLOCK : top + (c + 1) * BLOCK, :],
            kv_ref[c * CHUNK : (c + 1) * CHUNK, :],
        )
    rows = pl.ds(half.local(edge), BLOCK)
    lse_ref[rows, :] = jnp.broadcast_to(peak + jnp.log(total), (BLOCK, 128))
    o_ref[rows, :] = low(out * (1.0 / total))

    def output(i, c):
        j = half.middle(i)
        rows = pl.ds(pl.multiple_of(i * BLOCK, BLOCK), BLOCK)
        out = dot(p_ref[rows, :], gather(j)[1]) * l_ref[rows, :]
        o_ref[pl.ds(half.local(j), BLOCK), :] = low(out)
        return c

    lax.fori_loop(0, count, output, 0, unroll=count)


def attention_forward(meta, rand, proj, segq, segtab, segrow, other):
    n = proj.shape[0]
    heads = proj.shape[1] // 256
    nblk = n // BLOCK
    rows = n // 2
    tall = (nblk // 2 - 1 + n // CHUNK) * BLOCK
    col = lambda h, *_: (0, h)
    fix = lambda h, *_: (0, 0)
    part = pl.BlockSpec((rows, 128), col)
    return pl.pallas_call(
        functools.partial(fwd_kernel, nblk=nblk, other=other),
        out_shape=(
            jax.ShapeDtypeStruct((rows, heads * 128), jnp.bfloat16),
            jax.ShapeDtypeStruct((rows, heads * 128), jnp.float32),
        ),
        grid_spec=pltpu.PrefetchScalarGridSpec(
            num_scalar_prefetch=2,
            grid=(heads,),
            in_specs=[
                pl.BlockSpec((n, 128), col),
                pl.BlockSpec((n, 128), lambda h, *_: (0, heads + h)),
                pl.BlockSpec(segq.shape, fix),
                pl.BlockSpec(segtab.shape, fix),
                pl.BlockSpec(segrow.shape, fix),
            ],
            out_specs=[part, part],
            scratch_shapes=[
                pltpu.VMEM((tall, CHUNK), jnp.float32),
                pltpu.VMEM((tall, CHUNK), jnp.bfloat16),
                pltpu.VMEM((tall, 128), jnp.float32),
            ],
        ),
        cost_estimate=pl.CostEstimate(
            flops=8 * heads * rows * CHUNK * 128,
            bytes_accessed=heads * n * 128 * 6,
            transcendentals=heads * rows * CHUNK,
        ),
        name="attn_fwd",
    )(meta, rand, proj, proj, segq, segtab, segrow)


def bwd_kernel(
    meta_ref, rand_ref, q_ref, kv_ref, do_ref, o_ref, lse_ref, segq_ref, segtab_ref, segrow_ref,
    *rest, nblk, other, chained,
):
    if chained:
        prior_ref, dq_ref, dkv_ref, acc_ref, sd_ref, ds_ref = rest
    else:
        dq_ref, dkv_ref, acc_ref, sd_ref, ds_ref = rest
    head = pl.program_id(0)
    half = Half(meta_ref, other, nblk)
    count = nblk // 2 - 1
    chunks = nblk * BLOCK // CHUNK
    pair = 2 * BLOCK
    top = count * pair
    acc_ref[...] = prior_ref[...] if chained else jnp.zeros_like(acc_ref)
    right = lax.broadcasted_iota(jnp.int32, (BLOCK, 128), 1) >= HEAD_DIM

    def gather(j):
        blocks = slot_blocks(rand_ref, head, j, nblk)
        keys = jnp.concatenate([kv_ref[pl.ds(half.place(b), BLOCK), :] for b in blocks], axis=0)
        return blocks, keys

    def stacked(j):
        return jnp.concatenate(
            [q_ref[pl.ds(half.place(j), BLOCK), :], do_ref[pl.ds(half.local(j), BLOCK), :]], axis=0
        )

    def delta_of(j):
        rows = pl.ds(half.local(j), BLOCK)
        product = wide(do_ref[rows, :]) * wide(o_ref[rows, :])
        return jnp.sum(jnp.where(right, product, 0.0), axis=1, keepdims=True)

    def segq_of(j):
        return tile4(segq_ref[pl.ds(pl.multiple_of(j * BLOCK, BLOCK), BLOCK), :])

    def lse_of(j):
        return tile4(lse_ref[pl.ds(half.local(j), BLOCK), :])

    def score(i, c):
        j = half.middle(i)
        blocks, keys = gather(j)
        sd = dot(stacked(j), keys, NT)
        ok = segq_of(j) == slot_segments(segtab_ref, blocks, j, nblk)
        sd_ref[pl.ds(pl.multiple_of(i * pair, pair), BLOCK), :] = jnp.where(
            ok, sd[:BLOCK], NEG_FILL
        )
        sd_ref[pl.ds(pl.multiple_of(i * pair + BLOCK, BLOCK), BLOCK), :] = sd[BLOCK:]
        return c

    lax.fori_loop(0, count, score, 0, unroll=count)
    edge = half.edge()
    edge_pair = stacked(edge)
    seg_edge = segq_of(edge)
    for c in range(chunks):
        sd = dot(edge_pair, kv_ref[c * CHUNK : (c + 1) * CHUNK, :], NT)
        seg = segrow_ref[pl.ds(c ^ meta_ref[2], 1), :]
        row = top + c * pair
        sd_ref[row : row + BLOCK, :] = jnp.where(seg_edge == seg, sd[:BLOCK], NEG_FILL)
        sd_ref[row + BLOCK : row + pair, :] = sd[BLOCK:]

    def soften(row, lse, delta):
        p = jnp.exp(sd_ref[pl.ds(row, BLOCK), :] - lse)
        ds_ref[pl.ds(row + BLOCK, BLOCK), :] = low(p)
        ds_ref[pl.ds(row, BLOCK), :] = low(p * (sd_ref[pl.ds(row + BLOCK, BLOCK), :] - delta))

    def soften_middle(i, c):
        j = half.middle(i)
        soften(pl.multiple_of(i * pair, pair), lse_of(j), delta_of(j))
        return c

    lax.fori_loop(0, count, soften_middle, 0, unroll=count)
    lse = lse_of(edge)
    delta = delta_of(edge)
    for c in range(chunks):
        soften(top + c * pair, lse, delta)

    def spread(i, c):
        j = half.middle(i)
        blocks, keys = gather(j)
        dsp = ds_ref[pl.ds(pl.multiple_of(i * pair, pair), pair), :]
        dq_ref[pl.ds(half.local(j), BLOCK), :] = low(dot(dsp[:BLOCK], keys))
        dkv = dot(dsp, stacked(j), TN)
        places = [pl.ds(half.place(b), BLOCK) for b in blocks]
        olds = [acc_ref[place, :] for place in places]
        for s in (2, 3, 4, 5, 6, 7, 0, 1):
            acc_ref[places[s], :] = olds[s] + dkv[s * BLOCK : (s + 1) * BLOCK]
        return c

    lax.fori_loop(0, count, spread, 0, unroll=count)
    dq = jnp.zeros((BLOCK, 128), jnp.float32)
    for c in range(chunks):
        dsp = ds_ref[top + c * pair : top + (c + 1) * pair, :]
        dq = dq + dot(dsp[:BLOCK], kv_ref[c * CHUNK : (c + 1) * CHUNK, :])
        acc_ref[c * CHUNK : (c + 1) * CHUNK, :] += dot(dsp, edge_pair, TN)
    dq_ref[pl.ds(half.local(edge), BLOCK), :] = low(dq)
    dkv_ref[...] = acc_ref[...].astype(dkv_ref.dtype)


def attention_backward(meta, rand, proj, do, out, lse, segq, segtab, segrow, other, prior, kind):
    n = proj.shape[0]
    heads = proj.shape[1] // 256
    nblk = n // BLOCK
    rows = n // 2
    tall = (nblk // 2 - 1 + n // CHUNK) * BLOCK * 2
    col = lambda h, *_: (0, h)
    fix = lambda h, *_: (0, 0)
    full = pl.BlockSpec((n, 128), col)
    part = pl.BlockSpec((rows, 128), col)
    specs = [
        full,
        pl.BlockSpec((n, 128), lambda h, *_: (0, heads + h)),
        part,
        part,
        part,
        pl.BlockSpec(segq.shape, fix),
        pl.BlockSpec(segtab.shape, fix),
        pl.BlockSpec(segrow.shape, fix),
    ]
    operands = [meta, rand, proj, proj, do, out, lse, segq, segtab, segrow]
    if prior is not None:
        specs.append(full)
        operands.append(prior)
    return pl.pallas_call(
        functools.partial(bwd_kernel, nblk=nblk, other=other, chained=prior is not None),
        out_shape=(
            jax.ShapeDtypeStruct((rows, heads * 128), jnp.bfloat16),
            jax.ShapeDtypeStruct((n, heads * 128), kind),
        ),
        grid_spec=pltpu.PrefetchScalarGridSpec(
            num_scalar_prefetch=2,
            grid=(heads,),
            in_specs=specs,
            out_specs=[part, full],
            scratch_shapes=[
                pltpu.VMEM((n, 128), jnp.float32),
                pltpu.VMEM((tall, CHUNK), jnp.float32),
                pltpu.VMEM((tall, CHUNK), jnp.bfloat16),
            ],
        ),
        cost_estimate=pl.CostEstimate(
            flops=16 * heads * rows * CHUNK * 128,
            bytes_accessed=heads * n * 128 * 10,
            transcendentals=heads * rows * CHUNK,
        ),
        name="attn_bwd",
    )(*operands)


def ffn_kernel(x_ref, g_ref, up_ref, down_ref, bias_ref, out_ref, dx_ref, act_ref, dpre_ref, sum_ref):
    pre = dot(x_ref[...], up_ref[...]) + bias_ref[...]
    cumulative = 0.5 * (1.0 + lax.erf(pre * INV_ROOT_TWO))
    act = low(pre * cumulative)
    act_ref[...] = act
    out_ref[...] = low(dot(act, down_ref[...], NT))
    slope = cumulative + pre * jnp.exp(-0.5 * pre * pre) * INV_ROOT_TWO_PI
    dpre = low(dot(g_ref[...], down_ref[...]) * slope)
    dpre_ref[...] = dpre
    dx_ref[...] = low(dot(dpre, up_ref[...], NT))

    @pl.when(pl.program_id(0) == 0)
    def _():
        sum_ref[...] = jnp.zeros_like(sum_ref)

    sum_ref[...] += jnp.sum(wide(dpre), axis=0, keepdims=True)


def feed_forward(x, g, up, down, bias, tile=256):
    rows, width = x.shape
    cols = up.shape[1]
    row = lambda i: (i, 0)
    fix = lambda i: (0, 0)
    return pl.pallas_call(
        ffn_kernel,
        out_shape=(
            jax.ShapeDtypeStruct((rows, width), jnp.bfloat16),
            jax.ShapeDtypeStruct((rows, width), jnp.bfloat16),
            jax.ShapeDtypeStruct((rows, cols), jnp.bfloat16),
            jax.ShapeDtypeStruct((rows, cols), jnp.bfloat16),
            jax.ShapeDtypeStruct((1, cols), jnp.float32),
        ),
        grid=(rows // tile,),
        in_specs=[
            pl.BlockSpec((tile, width), row),
            pl.BlockSpec((tile, width), row),
            pl.BlockSpec(up.shape, fix),
            pl.BlockSpec(down.shape, fix),
            pl.BlockSpec(bias.shape, fix),
        ],
        out_specs=[
            pl.BlockSpec((tile, width), row),
            pl.BlockSpec((tile, width), row),
            pl.BlockSpec((tile, cols), row),
            pl.BlockSpec((tile, cols), row),
            pl.BlockSpec((1, cols), fix),
        ],
        cost_estimate=pl.CostEstimate(
            flops=8 * rows * width * cols,
            bytes_accessed=12 * rows * width,
            transcendentals=2 * rows * cols,
        ),
        name="ffn",
    )(x, g, up, down, bias)


def swap(v, axis, size, stride):
    return lax.ppermute(v, axis, [(i, i ^ stride) for i in range(size)])


def after(v, *others):
    return lax.optimization_barrier((v,) + others)[0]


def strides_of(size):
    out = []
    while size > 1:
        size //= 2
        out.append(size)
    return out


class Group:
    def __init__(self, axis, size):
        self.axis = axis
        self.size = size
        self.index = lax.axis_index(axis)
        self.strides = strides_of(size)

    def bit(self, stride):
        return (self.index // stride) % 2

    def swap(self, v, stride):
        return swap(v, self.axis, self.size, stride)

    def gather_step(self, v, stride):
        got = self.swap(v, stride)
        return jnp.where(self.bit(stride) == 0, jnp.stack([v, got]), jnp.stack([got, v]))

    def gather_finish(self, v, order):
        held = list(reversed(order))
        k = len(held)
        perm = sorted(range(k), key=lambda a: -held[a])
        v = v.transpose(perm + list(range(k, v.ndim)))
        return v.reshape((-1,) + v.shape[k + 1 :])

    def scatter_start(self, v):
        k = len(self.strides)
        return v.reshape((2,) * k + (v.shape[0] // self.size,) + v.shape[1:])

    def scatter_step(self, v, stride, held):
        at = held.index(stride)
        bit = self.bit(stride)
        send = low(lax.dynamic_index_in_dim(v, 1 - bit, at, keepdims=False))
        keep = wide(lax.dynamic_index_in_dim(v, bit, at, keepdims=False))
        return keep + wide(self.swap(send, stride)), [s for s in held if s != stride]

    def scatter(self, v, order):
        v = self.scatter_start(v)
        held = list(self.strides)
        for stride in order:
            v, held = self.scatter_step(v, stride, held)
        return v

    def total(self, v):
        for stride in reversed(self.strides):
            v = v + self.swap(v, stride)
        return v


def norm_stats(values):
    average = jnp.mean(values, axis=-1, keepdims=True)
    centered = values - average
    variance = jnp.mean(centered * centered, axis=-1, keepdims=True)
    inverse = lax.rsqrt(variance + NORM_EPS)
    return (centered * inverse, inverse)


def norm_back(grad_output, normed, inverse, gain_row):
    scaled = grad_output * gain_row
    return inverse * (
        scaled
        - jnp.mean(scaled, axis=-1, keepdims=True)
        - normed * jnp.mean(scaled * normed, axis=-1, keepdims=True)
    )


def split_heads(v):
    return v.reshape(v.shape[0], -1, HEAD_DIM)


def pad_right(v):
    v = split_heads(v)
    return jnp.concatenate([v, jnp.zeros_like(v)], axis=2).reshape(v.shape[0], -1)


def pad_left(v):
    v = split_heads(v)
    return jnp.concatenate([jnp.zeros_like(v), v], axis=2).reshape(v.shape[0], -1)


def left_halves(v):
    return v.reshape(v.shape[0], -1, 128)[:, :, :HEAD_DIM].reshape(v.shape[0], -1)


def right_halves(v):
    return v.reshape(v.shape[0], -1, 128)[:, :, HEAD_DIM:].reshape(v.shape[0], -1)


def interleave(a, b):
    return jnp.concatenate([split_heads(a), split_heads(b)], axis=2).reshape(a.shape[0], -1)


def local(
    tokens, cotangent, segment_ids, rand_blocks, w_qkv, qv_bias, w_out, w_up, up_bias, w_down,
    norm_gain, norm_bias, branch_bias, *, dp, mp,
):
    dpg = Group("dp", dp)
    mpg = Group("mp", mp)
    me = mpg.index
    CORE, CHIP = 1, 2
    rows = tokens.shape[0]
    width = tokens.shape[1]
    cols = w_qkv.shape[2]
    gains, shifts, branch_shift = wide(norm_gain), wide(norm_bias), wide(branch_bias)

    inputs = wide(tokens)
    normed_one, inverse_one = norm_stats(inputs)
    act_one = low(normed_one * gains[0] + shifts[0])
    act_far = mpg.swap(act_one, CHIP)
    act_near = mpg.swap(act_one, CORE)
    act_last = mpg.swap(act_far, CORE)
    act_one_all = jnp.concatenate([act_one, act_near, act_far, act_last], axis=0)

    far_first = dpg.strides
    near_first = [1] + dpg.strides[:-1]
    small = w_qkv.transpose(1, 0, 2).reshape(w_qkv.shape[1], 3 * cols)
    for stride in far_first:
        small = dpg.gather_step(small, stride)
    qkv = dpg.gather_finish(small, far_first)
    w_proj = jnp.concatenate(
        [
            pad_right(qkv[:, :cols] * jnp.bfloat16(SCALE)),
            interleave(qkv[:, cols : 2 * cols], qkv[:, 2 * cols :]),
        ],
        axis=1,
    )
    shift_q = wide(qv_bias[0:1]) * SCALE
    shift_v = wide(qv_bias[1:2])
    b_proj = jnp.concatenate([pad_right(shift_q), pad_left(shift_v)], axis=1)

    mixed = jnp.concatenate([w_up, w_out.T], axis=1)
    mixed = after(mixed, small)
    for stride in far_first:
        mixed = dpg.gather_step(mixed, stride)
    mixed = dpg.gather_finish(mixed, far_first)
    full_up = mixed[:, : w_up.shape[1]]
    out_mine = mixed[:, w_up.shape[1] :]
    down = dpg.gather_step(w_down.T, 1)
    down = after(down, mixed)
    for stride in near_first[1:]:
        down = dpg.gather_step(down, stride)
    full_down = dpg.gather_finish(down, near_first)

    cot_far = mpg.swap(after(cotangent, act_far), CHIP)
    cot_near = mpg.swap(cotangent, CORE)
    cot_last = mpg.swap(cot_far, CORE)
    cot_here = jnp.concatenate([cotangent, cot_near], axis=0)
    cot_there = jnp.concatenate([cot_far, cot_last], axis=0)

    proj = low(dot(act_one_all, w_proj) + b_proj)

    seg = segment_ids[0]
    nblk = seg.shape[0] // BLOCK
    segq = jnp.broadcast_to(seg[:, None], (seg.shape[0], 128))
    blocks = seg.reshape(nblk, BLOCK)
    segtab = jnp.concatenate([blocks, blocks], axis=1)
    segrow = seg.reshape(-1, CHUNK)
    meta = jnp.stack([me * (nblk // mp), me // 2, me]).astype(jnp.int32)
    rand = rand_blocks.reshape(-1)
    chip_rows = 2 * rows
    o_there, lse_there = attention_forward(meta, rand, proj, segq, segtab, segrow, 1)
    merged_there = right_halves(o_there)
    merged_got = mpg.swap(merged_there, CHIP)
    o_here, lse_here = attention_forward(meta, rand, proj, segq, segtab, segrow, 0)
    out_yours = mpg.swap(out_mine, CHIP)
    out_both = jnp.concatenate([out_mine, out_yours], axis=1)
    merged = jnp.concatenate([right_halves(o_here), merged_got], axis=1)
    attn = low(dot(merged, out_both, NT))
    attn_near = mpg.swap(attn[rows:], CORE)
    hidden = inputs + (wide(attn[:rows]) + wide(attn_near)) + branch_shift[0]

    normed_two, inverse_two = norm_stats(hidden)
    act_two = low(normed_two * gains[1] + shifts[1])
    two_far = mpg.swap(act_two, CHIP)
    two_near = mpg.swap(act_two, CORE)
    two_last = mpg.swap(two_far, CORE)
    two_here = jnp.concatenate([act_two, two_near], axis=0)
    two_there = jnp.concatenate([two_far, two_last], axis=0)
    bias = wide(up_bias)[None, :]
    ffn_a, dx_a, act_a, dpre_a, sum_a = feed_forward(two_here, cot_here, full_up, full_down, bias)
    ffn_b, dx_b, act_b, dpre_b, sum_b = feed_forward(two_there, cot_there, full_up, full_down, bias)

    def owners(here, there):
        near_here = mpg.swap(here[rows:], CORE)
        near_there = mpg.swap(there[rows:], CORE)
        mine = wide(here[:rows]) + wide(near_here)
        far = mpg.swap(low(wide(there[:rows]) + wide(near_there)), CHIP)
        return mine + wide(far), far

    grad_act_two, dx_far = owners(dx_a, dx_b)
    grad_top = wide(cotangent)
    grad_hidden = grad_top + norm_back(grad_act_two, normed_two, inverse_two, gains[1])
    grad_low = low(grad_hidden)
    grad_up_part = dot(two_here, dpre_a, TN) + dot(two_there, dpre_b, TN)
    grad_down_part = dot(cot_here, act_a, TN) + dot(cot_there, act_b, TN)

    low_near = mpg.swap(grad_low, CORE)
    hid_here = jnp.concatenate([grad_low, low_near], axis=0)
    do_there_out = low(dot(hid_here, out_yours))
    do_got = mpg.swap(do_there_out, CHIP)
    do_here = low(dot(hid_here, pad_left(out_mine)))
    dq_here, dkv_part = attention_backward(
        meta, rand, proj, do_here, o_here, lse_here, segq, segtab, segrow, 0, None, jnp.float32
    )
    ffn_rows, _ = owners(ffn_a, after(ffn_b, do_got))
    layer_out = low(hidden + ffn_rows + branch_shift[1])
    dq_there, dkv = attention_backward(
        meta, rand, proj, pad_left(do_got), o_there, lse_there, segq, segtab, segrow, 1,
        dkv_part, jnp.bfloat16,
    )
    w_q, w_kv = w_proj[:, : 2 * cols], w_proj[:, 2 * cols :]
    one_there = low(dot(dq_there, w_q, NT) + dot(dkv[chip_rows:], w_kv, NT))
    one_here = low(dot(dq_here, w_q, NT) + dot(dkv[:chip_rows], w_kv, NT))
    grad_act_one, _ = owners(one_here, one_there)
    input_grad = grad_hidden + norm_back(grad_act_one, normed_one, inverse_one, gains[0])

    grad_out_pair = dot(hid_here, merged, TN)
    grad_out_got = mpg.swap(low(grad_out_pair[:, cols:]), CHIP)
    grad_out_part = grad_out_pair[:, :cols] + wide(grad_out_got)
    near_up = list(reversed(far_first))
    down_order = list(reversed(near_first))
    grad_down_own = dpg.scatter(grad_down_part, down_order)
    up_out = dpg.scatter(jnp.concatenate([grad_up_part, grad_out_part], axis=1), near_up)
    dq_all = jnp.concatenate([dq_here, dq_there], axis=0)
    grad_q = left_halves(dot(act_one_all, dq_all, TN)) * SCALE
    grad_kv = dot(act_one_all, dkv, TN)
    grad_proj = jnp.concatenate([grad_q, left_halves(grad_kv), right_halves(grad_kv)], axis=1)
    grad_proj = dpg.scatter(grad_proj, near_up)
    grad_qkv = grad_proj.reshape(-1, 3, cols).transpose(1, 0, 2)

    one_all = wide(jnp.concatenate([one_here, one_there], axis=0))
    normed_all = (wide(act_one_all) - shifts[0]) / gains[0]
    sum_q = left_halves(jnp.sum(wide(dq_all), axis=0, keepdims=True)) * SCALE
    sum_v = right_halves(jnp.sum(wide(dkv), axis=0, keepdims=True))
    qv = jnp.concatenate([sum_q, sum_v], axis=1)
    qv = jnp.pad(qv, ((0, 0), (0, width - qv.shape[1])))
    sums = jnp.concatenate(
        [
            jnp.sum(one_all * normed_all, axis=0, keepdims=True),
            jnp.sum(grad_act_two * normed_two, axis=0, keepdims=True),
            jnp.sum(one_all, axis=0, keepdims=True),
            jnp.sum(grad_act_two, axis=0, keepdims=True),
            jnp.sum(grad_hidden, axis=0, keepdims=True),
            jnp.sum(grad_top, axis=0, keepdims=True),
            sum_a + sum_b,
            qv,
        ],
        axis=0,
    )
    sums = dpg.total(sums)
    norms = mpg.total(sums[:6])
    return (
        layer_out,
        input_grad,
        grad_qkv,
        sums[7, : 2 * cols].reshape(2, cols),
        up_out[:, w_up.shape[1] :].T,
        up_out[:, : w_up.shape[1]],
        sums[6],
        grad_down_own.T,
        norms[0:2],
        norms[2:4],
        norms[4:6],
    )


def solution(mesh):
    in_specs = (
        P(("dp", "mp"), None),
        P(("dp", "mp"), None),
        P("dp", None),
        P("dp", "mp", None, None),
        P(None, "dp", "mp"),
        P(None, "mp"),
        P("mp", "dp"),
        P("dp", "mp"),
        P("mp"),
        P("mp", "dp"),
        P(),
        P(),
        P(),
    )
    out_specs = (
        P(("dp", "mp"), None),
        P(("dp", "mp"), None),
        P(None, "dp", "mp"),
        P(None, "mp"),
        P("mp", "dp"),
        P("dp", "mp"),
        P("mp"),
        P("mp", "dp"),
        P(),
        P(),
        P(),
    )
    body = functools.partial(local, dp=mesh.shape["dp"], mp=mesh.shape["mp"])
    return jax.shard_map(body, mesh=mesh, in_specs=in_specs, out_specs=out_specs, check_vma=False)
```
